32 devices in a mesh: slab: 4 (over x, core), chan: 8 (over z, y).
Axes of the slice: x: 2, y: 2, z: 4, core: 2. Of those that a mesh axis runs over, the one named last changes fastest.
Arguments:
- inputs: bfloat16 [512, 32, 256], P('chan', 'slab'), may hold values from -6 to 6
- weights: bfloat16 [27, 512, 512], P(None, 'chan', 'slab'), may hold values from -0.0546875 to 0.0546875
- cotangent: bfloat16 [512, 32, 256], P('chan', 'slab'), may hold values from -6 to 6
Outputs:
- outputs: bfloat16 [512, 32, 256], P('chan', 'slab')
- gradient: bfloat16 [512, 32, 256], P('chan', 'slab')
The draws below stay inside these ranges and needn't reach their ends.
All inputs are finite; a program needn't handle non-finite values.
Results may differ from the reference program's by a relative error of at most 0.0014.
Values may be sent and summed in bfloat16 or wider, within the bound.
A program may use at most 64 MiB of HBM per device.

```python
import jax
import jax.numpy as jnp
from jax import lax

C = 512
ROWS = 8
COLS = 32
DEPTH = 32


def block_scale(stream_key, dims, cuts, smallest, high):
    gain = 1.0
    for dim, blocks in cuts:
        steps = jax.random.uniform(jax.random.fold_in(jax.random.fold_in(stream_key, 6), dim), (blocks,), jnp.float32, smallest / len(cuts), high / len(cuts))
        gain = gain * jnp.repeat(jnp.exp(steps), dims[dim] // blocks).reshape((-1,) + (1,) * (len(dims) - 1 - dim))
    return gain


def bell_draw(stream_key, extent, scale, bound, shards=(), dtype=jnp.bfloat16):
    values = scale * jax.random.normal(stream_key, extent, jnp.float32)
    if shards:
        values = values * block_scale(stream_key, extent, shards, -0.22, 0.18)
    return jnp.clip(values, -bound, bound).astype(dtype)


def setup_inputs(seed: int = 0) -> dict:
    keys = jax.random.split(jax.random.key(seed), 4)
    inputs = bell_draw(keys[0], (C, DEPTH, ROWS * COLS), 1.0, 6.0, ((0, 8), (1, 4)))
    weights = bell_draw(keys[1], (27, C, C), (27 * C) ** -0.5, 0.0546875, ((1, 8), (2, 4)))
    cotangent = bell_draw(keys[2], (C, DEPTH, ROWS * COLS), 1.0, 6.0, ((0, 8), (1, 4)))
    return {"inputs": inputs, "weights": weights, "cotangent": cotangent}


def convolve(volume, kernel):
    channels = volume.shape[0]
    shaped = volume.reshape(1, channels, volume.shape[1], ROWS, COLS)
    filters = jnp.transpose(kernel, (1, 2, 0)).reshape(kernel.shape[1], kernel.shape[2], 3, 3, 3)
    result = lax.conv_general_dilated(shaped, filters, (1, 1, 1), ((1, 1), (1, 1), (1, 1)), dimension_numbers=('NCDHW', 'OIDHW', 'NCDHW'), precision=lax.Precision.HIGHEST)
    return result.reshape(kernel.shape[1], volume.shape[1], ROWS * COLS)

def reference(inputs, weights, cotangent):
    volume_in = inputs.astype(jnp.float32)
    kernel_in = weights.astype(jnp.float32)

    def forward(field_in):
        return convolve(field_in, kernel_in)
    result, pullback = jax.vjp(forward, volume_in)
    grad_in = pullback(cotangent.astype(jnp.float32))[0]
    return (result.astype(jnp.bfloat16), grad_in.astype(jnp.bfloat16))
```

```python
import functools

import jax
import jax.numpy as jnp
from jax import lax
from jax.experimental import pallas as pl
from jax.experimental.pallas import tpu as pltpu
from jax.sharding import PartitionSpec as P

ROWS = 8
COLS = 32
TAPS = 27
LANES = 128


def when(cond, fn):
    if cond is None:
        fn()
    else:
        pl.when(cond)(fn)


def both(a, b):
    return b if a is None else a if b is None else jnp.logical_and(a, b)


def gather_kernel(S, Z, Y, r, x_ref, w_ref, p_ref, g_ref, wf_ref, wg_ref,
                  lsem, vsend, ysend, vrecv, hsend, hrecv, wsend, wrecv, psend, fsend, precv):
    n = Z * Y
    planes = x_ref.shape[1]
    s, c = lax.axis_index("slab"), lax.axis_index("chan")
    z, y = lax.div(c, Y), lax.rem(c, Y)
    core = lax.rem(s, 2)
    mate = s + 1 - 2 * core
    ypeer = [z * Y + lax.rem(y + j, Y) for j in range(1, Y)]
    up, down = z < Z - 1, z > 0

    barrier = pltpu.get_barrier_semaphore()
    links = [(up, (s, c + Y)), (down, (s, c - Y))]
    links += [(None, (s, peer)) for peer in ypeer]
    links += [(None, (lax.rem(s + j, S), c)) for j in range(1, S)]
    targets = []
    for xx in range(S // 2):
        for j in range(r):
            to = (2 * xx + lax.rem(c, 2), s * r + j)
            targets.append((jnp.logical_or(to[0] != s, to[1] != c), to, j, xx * r + j))
    sources = []
    for k in range(n // 2):
        frm = (lax.div(c, r), 2 * k + core)
        sources.append((jnp.logical_or(frm[0] != s, frm[1] != c), frm))
    links += [(t[0], t[1]) for t in targets] + sources
    for cond, peer in links:
        when(cond, functools.partial(pl.semaphore_signal, barrier, inc=1, device_id=peer,
                                     device_id_type=pl.DeviceIdType.MESH))
    peers = sum(1 if cond is None else cond.astype(jnp.int32) for cond, _ in links)
    pl.semaphore_wait(barrier, peers)

    sent = []

    def send(cond, src, dst, ssem, rsem, to):
        def make():
            return pltpu.make_async_remote_copy(src_ref=src, dst_ref=dst, send_sem=ssem, recv_sem=rsem,
                                                device_id=to, device_id_type=pl.DeviceIdType.MESH)
        when(cond, lambda: make().start())
        sent.append((cond, make))

    def arrive(cond, dst, sem):
        when(cond, lambda: pltpu.make_async_copy(dst, dst, sem).wait())

    def block(v, slot):
        return g_ref.at[v, pl.ds(1, planes), slot]

    def along(cond, v, slot, src, side):
        ok, to = (up, (s, c + Y)) if side == 0 else (down, (s, c - Y))
        send(both(cond, ok), src, block(v, slot), vsend.at[v, side, slot], vrecv.at[v, slot], to)

    def across(cond, v, slot, src):
        for j, peer in enumerate(ypeer):
            send(cond, src, block(v, slot), ysend.at[v, j, slot], vrecv.at[v, slot], (s, peer))

    def halo(cond, v, slot, first, last):
        send(both(cond, s < S - 1), last, g_ref.at[v, 0, slot], hsend.at[v, 0, slot], hrecv.at[v, 0, slot], (s + 1, c))
        send(both(cond, s > 0), first, g_ref.at[v, planes + 1, slot], hsend.at[v, 1, slot], hrecv.at[v, 1, slot],
             (s - 1, c))

    def landed(cond, v, slot):
        arrive(cond, block(v, slot), vrecv.at[v, slot])

    def rim(cond, v, slot):
        halo(cond, v, slot, g_ref.at[v, 1, slot], g_ref.at[v, planes, slot])

    across(None, 1, c, x_ref.at[1])
    along(None, 0, c, x_ref.at[0], 0)
    along(None, 0, c, x_ref.at[0], 1)
    for cond, to, j, k in targets:
        send(cond, p_ref.at[j], wg_ref.at[c], psend.at[k], precv.at[c], to)
    along(None, 1, c, x_ref.at[1], 0)
    along(None, 1, c, x_ref.at[1], 1)
    across(None, 0, c, x_ref.at[0])
    for j in range(1, S):
        send(None, w_ref, wf_ref.at[s], wsend.at[j], wrecv.at[s], (lax.rem(s + j, S), c))
    for v in range(2):
        pltpu.make_async_copy(x_ref.at[v], block(v, c), lsem.at[v]).start()
        halo(None, v, c, x_ref.at[v, 0], x_ref.at[v, planes - 1])
    pltpu.make_async_copy(w_ref, wf_ref.at[s], lsem.at[2]).start()
    home = jnp.logical_and(s == lax.div(c, r), lax.rem(c, 2) == core)
    when(home, lambda: pltpu.make_async_copy(p_ref.at[lax.rem(c, r)], wg_ref.at[c], precv.at[c]).start())

    for side in range(2):
        def clear(side=side):
            for v in range(2):
                row = 0 if side == 0 else planes + 1
                g_ref[v, row] = jnp.zeros(g_ref.shape[2:], g_ref.dtype)
        when(s == (0 if side == 0 else S - 1), clear)

    for peer in ypeer:
        landed(None, 1, peer)
        along(None, 1, peer, block(1, peer), 0)
        along(None, 1, peer, block(1, peer), 1)
        rim(None, 1, peer)
    for k in range(1, Z):
        for side in range(2):
            zz = z - k if side == 0 else z + k
            have = zz >= 0 if side == 0 else zz < Z
            slot = zz * Y + y
            landed(have, 0, slot)
            if k < Z - 1:
                along(have, 0, slot, block(0, slot), side)
            across(have, 0, slot, block(0, slot))
            rim(have, 0, slot)
            for yy in range(Y):
                slot = zz * Y + yy
                landed(have, 1, slot)
                if k < Z - 1:
                    along(have, 1, slot, block(1, slot), side)
                rim(have, 1, slot)
    for k in range(n // 2):
        slot = 2 * k + core
        arrive(None, wg_ref.at[slot], precv.at[slot])
        send(None, wg_ref.at[slot], wg_ref.at[slot], fsend.at[k], precv.at[slot], (mate, c))
    for peer in ypeer:
        landed(None, 0, peer)
        rim(None, 0, peer)
        for k in range(1, Z):
            for side in range(2):
                zz = z - k if side == 0 else z + k
                have = zz >= 0 if side == 0 else zz < Z
                slot = zz * Y + peer - z * Y
                landed(have, 0, slot)
                rim(have, 0, slot)
    for v in range(2):
        pltpu.make_async_copy(x_ref.at[v], block(v, c), lsem.at[v]).wait()
    pltpu.make_async_copy(w_ref, wf_ref.at[s], lsem.at[2]).wait()
    for j in range(1, S):
        slot = lax.rem(s + j, S)
        arrive(None, wf_ref.at[slot], wrecv.at[slot])
    for k in range(n // 2):
        slot = 2 * k + 1 - core
        arrive(None, wg_ref.at[slot], precv.at[slot])
    for v in range(2):
        for slot in range(n):
            arrive(s > 0, g_ref.at[v, 0, slot], hrecv.at[v, 0, slot])
            arrive(s < S - 1, g_ref.at[v, planes + 1, slot], hrecv.at[v, 1, slot])
    for cond, make in sent:
        when(cond, lambda make=make: make().wait_send())


def conv_kernel(g_ref, wf_ref, wg_ref, o_ref, k_ref):
    S, _, lc, width = wf_ref.shape
    n = wg_ref.shape[0]
    planes = o_ref.shape[1]
    cells = o_ref.shape[3]
    pack = LANES // lc
    for t in range(TAPS):
        rows = pl.ds(t * lc, lc)
        k_ref[0, rows, :] = jnp.concatenate([wf_ref[i, t] for i in range(S)], axis=-1)
        at = (t % pack) * lc
        k_ref[1, rows, :] = jnp.concatenate([wg_ref[i, t // pack][:, at:at + lc] for i in range(n)], axis=-1)
    lane = lax.broadcasted_iota(jnp.int32, (lc, cells), 1)
    row, col = lane // COLS, lane % COLS
    nine = 9 * lc

    def step(k, carry):
        v, d = k // planes, k % planes
        total = None
        for a in range(3):
            part = jnp.dot(k_ref[v, pl.ds(a * nine, nine), :], g_ref[v, d + a], preferred_element_type=jnp.float32)
            total = part if total is None else total + part
        result = None
        for b in range(3):
            lines = None
            for c in range(3):
                at = (3 * b + c) * lc
                piece = total[at:at + lc]
                if c != 1:
                    piece = pltpu.roll(piece, (1 - c) % cells, 1)
                    piece = jnp.where(col == (0 if c == 0 else COLS - 1), 0.0, piece)
                lines = piece if lines is None else lines + piece
            if b != 1:
                lines = pltpu.roll(lines, ((1 - b) * COLS) % cells, 1)
                lines = jnp.where(row == (0 if b == 0 else ROWS - 1), 0.0, lines)
            result = lines if result is None else result + lines
        o_ref[v, d] = result.astype(o_ref.dtype)
        return carry

    lax.fori_loop(0, 2 * planes, step, 0)


def body(S, n, inputs, weights, cotangent):
    lc, planes, cells = inputs.shape
    wide = weights.shape[2]
    r = wide // lc
    C = n * lc
    Y = max(d for d in range(1, n + 1) if n % d == 0 and 2 * d * d <= n)
    Z = n // Y
    volumes = jnp.stack((inputs, cotangent)).transpose(0, 2, 1, 3)
    pack = LANES // lc
    nt = -(-TAPS // pack)
    flipped = jnp.pad(weights[::-1], ((0, nt * pack - TAPS), (0, 0), (0, 0)))
    pieces = flipped.reshape(nt, pack, lc, r, lc).transpose(3, 0, 4, 1, 2).reshape(r, nt, lc, pack * lc)
    vmem = pl.BlockSpec(memory_space=pltpu.VMEM)
    anyspace = pl.BlockSpec(memory_space=pl.ANY)
    dma = pltpu.SemaphoreType.DMA
    bf16 = jnp.bfloat16
    gathered, wf, wg = pl.pallas_call(
        functools.partial(gather_kernel, S, Z, Y, r),
        out_shape=(jax.ShapeDtypeStruct((2, planes + 2, n, lc, cells), bf16),
                   jax.ShapeDtypeStruct((S,) + weights.shape, bf16),
                   jax.ShapeDtypeStruct((n,) + pieces.shape[1:], bf16)),
        in_specs=[anyspace] * 3,
        out_specs=(vmem,) * 3,
        scratch_shapes=[dma((3,)), dma((2, 2, n)), dma((2, Y - 1, n)), dma((2, n)), dma((2, 2, n)), dma((2, 2, n)),
                        dma((S,)), dma((S,)), dma((S // 2 * r,)), dma((n // 2,)), dma((n,))],
        compiler_params=pltpu.CompilerParams(collective_id=0, has_side_effects=True, vmem_limit_bytes=40 << 20),
        name="gather",
    )(volumes, weights, pieces)
    out = pl.pallas_call(
        conv_kernel,
        out_shape=jax.ShapeDtypeStruct((2, planes, lc, cells), bf16),
        in_specs=[vmem] * 3,
        out_specs=vmem,
        scratch_shapes=[pltpu.VMEM((2, TAPS * lc, C), bf16)],
        compiler_params=pltpu.CompilerParams(vmem_limit_bytes=48 << 20),
        name="conv",
    )(gathered.reshape(2, planes + 2, C, cells), wf, wg)
    out = out.transpose(0, 2, 1, 3)
    return out[0], out[1]


def solution(mesh):
    S, n = mesh.shape["slab"], mesh.shape["chan"]
    return jax.shard_map(
        functools.partial(body, S, n),
        mesh=mesh,
        in_specs=(P("chan", "slab", None), P(None, "chan", "slab"), P("chan", "slab", None)),
        out_specs=(P("chan", "slab", None), P("chan", "slab", None)),
        check_vma=False,
    )
```

```python
import functools

import jax
import jax.numpy as jnp
from jax import lax
from jax.experimental import pallas as pl
from jax.experimental.pallas import tpu as pltpu
from jax.sharding import PartitionSpec as P

ROWS = 8
COLS = 32
TAPS = 27
LANES = 128
H = 2


def when(cond, fn):
    if cond is None:
        fn()
    else:
        pl.when(cond)(fn)


def both(a, b):
    return b if a is None else a if b is None else jnp.logical_and(a, b)


def gather_kernel(S, Z, Y, r, x_ref, w_ref, p_ref, g_ref, wf_ref, wg_ref,
                  lsem, vsend, ysend, vrecv, hsend, hrecv, wsend, wrecv, psend, fsend, precv):
    n = Z * Y
    planes = x_ref.shape[1]
    units, part = 2 * H, planes // H
    s, c = lax.axis_index("slab"), lax.axis_index("chan")
    z, y = lax.div(c, Y), lax.rem(c, Y)
    core = lax.rem(s, 2)
    mate = s + 1 - 2 * core
    ypeer = [z * Y + lax.rem(y + j, Y) for j in range(1, Y)]
    up, down = z < Z - 1, z > 0

    barrier = pltpu.get_barrier_semaphore()
    links = [(up, (s, c + Y)), (down, (s, c - Y))]
    links += [(None, (s, peer)) for peer in ypeer]
    links += [(None, (lax.rem(s + j, S), c)) for j in range(1, S)]
    targets = []
    for xx in range(S // 2):
        for j in range(r):
            to = (2 * xx + lax.rem(c, 2), s * r + j)
            targets.append((jnp.logical_or(to[0] != s, to[1] != c), to, j, xx * r + j))
    sources = []
    for k in range(n // 2):
        frm = (lax.div(c, r), 2 * k + core)
        sources.append((jnp.logical_or(frm[0] != s, frm[1] != c), frm))
    links += [(t[0], t[1]) for t in targets] + sources
    for cond, peer in links:
        when(cond, functools.partial(pl.semaphore_signal, barrier, inc=1, device_id=peer,
                                     device_id_type=pl.DeviceIdType.MESH))
    peers = sum(1 if cond is None else cond.astype(jnp.int32) for cond, _ in links)
    pl.semaphore_wait(barrier, peers)

    sent = []

    def send(cond, src, dst, ssem, rsem, to):
        def make():
            return pltpu.make_async_remote_copy(src_ref=src, dst_ref=dst, send_sem=ssem, recv_sem=rsem,
                                                device_id=to, device_id_type=pl.DeviceIdType.MESH)
        when(cond, lambda: make().start())
        sent.append((cond, make))

    def arrive(cond, dst, sem):
        when(cond, lambda: pltpu.make_async_copy(dst, dst, sem).wait())

    def own(u):
        return x_ref.at[u // H, pl.ds(u % H * part, part)]

    def block(u, slot):
        return g_ref.at[u // H, pl.ds(1 + u % H * part, part), slot]

    def along(cond, u, slot, src, side):
        ok, to = (up, (s, c + Y)) if side == 0 else (down, (s, c - Y))
        send(both(cond, ok), src, block(u, slot), vsend.at[u, side, slot], vrecv.at[u, slot], to)

    def across(cond, u, slot, src):
        for j, peer in enumerate(ypeer):
            send(cond, src, block(u, slot), ysend.at[u, j, slot], vrecv.at[u, slot], (s, peer))

    def landed(cond, u, slot):
        arrive(cond, block(u, slot), vrecv.at[u, slot])

    def rim(cond, u, slot, first=None, last=None):
        v = u // H
        if u % H == H - 1:
            last = g_ref.at[v, planes, slot] if last is None else last
            send(both(cond, s < S - 1), last, g_ref.at[v, 0, slot], hsend.at[v, 0, slot], hrecv.at[v, 0, slot],
                 (s + 1, c))
        if u % H == 0:
            first = g_ref.at[v, 1, slot] if first is None else first
            send(both(cond, s > 0), first, g_ref.at[v, planes + 1, slot], hsend.at[v, 1, slot], hrecv.at[v, 1, slot],
                 (s - 1, c))

    for u in range(units):
        for side in range(2):
            along(None, u, c, own(u), side)
        across(None, u, c, own(u))
        if u == H - 1:
            for cond, to, j, k in targets:
                send(cond, p_ref.at[j], wg_ref.at[c], psend.at[k], precv.at[c], to)
    for j in range(1, S // 2):
        send(None, w_ref, wf_ref.at[s], wsend.at[j], wrecv.at[s], (lax.rem(s + 2 * j, S), c))
    send(None, w_ref, wf_ref.at[s], wsend.at[0], wrecv.at[s], (mate, c))
    for u in range(units):
        pltpu.make_async_copy(own(u), block(u, c), lsem.at[u]).start()
        rim(None, u, c, x_ref.at[u // H, 0], x_ref.at[u // H, planes - 1])
    pltpu.make_async_copy(w_ref, wf_ref.at[s], lsem.at[units]).start()
    home = jnp.logical_and(s == lax.div(c, r), lax.rem(c, 2) == core)
    when(home, lambda: pltpu.make_async_copy(p_ref.at[lax.rem(c, r)], wg_ref.at[c], precv.at[c]).start())

    for side in range(2):
        def clear(side=side):
            for v in range(2):
                row = 0 if side == 0 else planes + 1
                g_ref[v, row] = jnp.zeros(g_ref.shape[2:], g_ref.dtype)
        when(s == (0 if side == 0 else S - 1), clear)

    for k in range(1, Z):
        for u in range(units):
            for side in range(2):
                zz = z - k if side == 0 else z + k
                have = zz >= 0 if side == 0 else zz < Z
                slot = zz * Y + y
                landed(have, u, slot)
                if k < Z - 1:
                    along(have, u, slot, block(u, slot), side)
                across(have, u, slot, block(u, slot))
                rim(have, u, slot)
        if k == 1:
            for j in range(1, S // 2):
                slot = lax.rem(s + 2 * j, S)
                arrive(None, wf_ref.at[slot], wrecv.at[slot])
                send(None, wf_ref.at[slot], wf_ref.at[slot], wsend.at[S // 2 + j], wrecv.at[slot], (mate, c))
    for k in range(n // 2):
        slot = 2 * k + core
        arrive(None, wg_ref.at[slot], precv.at[slot])
        send(None, wg_ref.at[slot], wg_ref.at[slot], fsend.at[k], precv.at[slot], (mate, c))
    for k in range(Z):
        for u in range(units):
            for peer in ypeer:
                for side in range(2 if k else 1):
                    zz = z - k if side == 0 else z + k
                    have = None if k == 0 else zz >= 0 if side == 0 else zz < Z
                    slot = zz * Y + peer - z * Y
                    landed(have, u, slot)
                    rim(have, u, slot)
    for u in range(units):
        pltpu.make_async_copy(own(u), block(u, c), lsem.at[u]).wait()
    pltpu.make_async_copy(w_ref, wf_ref.at[s], lsem.at[units]).wait()
    for j in range(S // 2):
        slot = lax.rem(mate + 2 * j, S)
        arrive(None, wf_ref.at[slot], wrecv.at[slot])
    for k in range(n // 2):
        slot = 2 * k + 1 - core
        arrive(None, wg_ref.at[slot], precv.at[slot])
    for v in range(2):
        for slot in range(n):
            arrive(s > 0, g_ref.at[v, 0, slot], hrecv.at[v, 0, slot])
            arrive(s < S - 1, g_ref.at[v, planes + 1, slot], hrecv.at[v, 1, slot])
    for cond, make in sent:
        when(cond, lambda make=make: make().wait_send())


def conv_kernel(g_ref, wf_ref, wg_ref, o_ref, k_ref):
    S, _, lc, width = wf_ref.shape
    n = wg_ref.shape[0]
    planes = o_ref.shape[1]
    cells = o_ref.shape[3]
    pack = LANES // lc
    for t in range(TAPS):
        rows = pl.ds(t * lc, lc)
        k_ref[0, rows, :] = jnp.concatenate([wf_ref[i, t] for i in range(S)], axis=-1)
        f = TAPS - 1 - t
        at = (f % pack) * lc
        k_ref[1, rows, :] = jnp.concatenate([wg_ref[i, f // pack][:, at:at + lc] for i in range(n)], axis=-1)
    lane = lax.broadcasted_iota(jnp.int32, (lc, cells), 1)
    row, col = lane // COLS, lane % COLS
    nine = 9 * lc

    def step(k, carry):
        v, d = k // planes, k % planes
        total = None
        for a in range(3):
            part = jnp.dot(k_ref[v, pl.ds(a * nine, nine), :], g_ref[v, d + a], preferred_element_type=jnp.float32)
            total = part if total is None else total + part
        result = None
        for b in range(3):
            lines = None
            for c in range(3):
                at = (3 * b + c) * lc
                piece = total[at:at + lc]
                if c != 1:
                    piece = pltpu.roll(piece, (1 - c) % cells, 1)
                    piece = jnp.where(col == (0 if c == 0 else COLS - 1), 0.0, piece)
                lines = piece if lines is None else lines + piece
            if b != 1:
                lines = pltpu.roll(lines, ((1 - b) * COLS) % cells, 1)
                lines = jnp.where(row == (0 if b == 0 else ROWS - 1), 0.0, lines)
            result = lines if result is None else result + lines
        o_ref[v, d] = result.astype(o_ref.dtype)
        return carry

    lax.fori_loop(0, 2 * planes, step, 0)


def body(S, n, inputs, weights, cotangent):
    lc, planes, cells = inputs.shape
    wide = weights.shape[2]
    r = wide // lc
    C = n * lc
    Y = max(d for d in range(1, n + 1) if n % d == 0 and 2 * d * d <= n)
    Z = n // Y
    volumes = jnp.stack((inputs, cotangent)).transpose(0, 2, 1, 3)
    pack = LANES // lc
    nt = -(-TAPS // pack)
    padded = jnp.pad(weights, ((0, nt * pack - TAPS), (0, 0), (0, 0)))
    pieces = padded.reshape(nt, pack, lc, r, lc).transpose(3, 0, 4, 1, 2).reshape(r, nt, lc, pack * lc)
    vmem = pl.BlockSpec(memory_space=pltpu.VMEM)
    anyspace = pl.BlockSpec(memory_space=pl.ANY)
    dma = pltpu.SemaphoreType.DMA
    bf16 = jnp.bfloat16
    gathered, wf, wg = pl.pallas_call(
        functools.partial(gather_kernel, S, Z, Y, r),
        out_shape=(jax.ShapeDtypeStruct((2, planes + 2, n, lc, cells), bf16),
                   jax.ShapeDtypeStruct((S,) + weights.shape, bf16),
                   jax.ShapeDtypeStruct((n,) + pieces.shape[1:], bf16)),
        in_specs=[anyspace] * 3,
        out_specs=(vmem,) * 3,
        scratch_shapes=[dma((2 * H + 1,)), dma((2 * H, 2, n)), dma((2 * H, Y - 1, n)), dma((2 * H, n)), dma((2, 2, n)), dma((2, 2, n)),
                        dma((S,)), dma((S,)), dma((S // 2 * r,)), dma((n // 2,)), dma((n,))],
        compiler_params=pltpu.CompilerParams(collective_id=0, has_side_effects=True, vmem_limit_bytes=40 << 20),
        name="gather",
    )(volumes, weights, pieces)
    out = pl.pallas_call(
        conv_kernel,
        out_shape=jax.ShapeDtypeStruct((2, planes, lc, cells), bf16),
        in_specs=[vmem] * 3,
        out_specs=vmem,
        scratch_shapes=[pltpu.VMEM((2, TAPS * lc, C), bf16)],
        compiler_params=pltpu.CompilerParams(vmem_limit_bytes=48 << 20),
        name="conv",
    )(gathered.reshape(2, planes + 2, C, cells), wf, wg)
    out = out.transpose(0, 2, 1, 3)
    return out[0], out[1]


def solution(mesh):
    S, n = mesh.shape["slab"], mesh.shape["chan"]
    return jax.shard_map(
        functools.partial(body, S, n),
        mesh=mesh,
        in_specs=(P("chan", "slab", None), P(None, "chan", "slab"), P("chan", "slab", None)),
        out_specs=(P("chan", "slab", None), P("chan", "slab", None)),
        check_vma=False,
    )
```

```python
import functools

import jax
import jax.numpy as jnp
from jax import lax
from jax.experimental import pallas as pl
from jax.experimental.pallas import tpu as pltpu
from jax.sharding import PartitionSpec as P

ROWS = 8
COLS = 32
TAPS = 27
LANES = 128
H = 2


def when(cond, fn):
    if cond is None:
        fn()
    else:
        pl.when(cond)(fn)


def both(a, b):
    return b if a is None else a if b is None else jnp.logical_and(a, b)


def gather_kernel(S, Z, Y, r, x_ref, w_ref, p_ref, g_ref, wf_ref, wg_ref,
                  lsem, vsend, ysend, vrecv, hsend, hrecv, wsend, wrecv, psend, fsend, xsend, precv):
    n = Z * Y
    planes = x_ref.shape[1]
    units, part = 2 * H, planes // H
    s, c = lax.axis_index("slab"), lax.axis_index("chan")
    z, y = lax.div(c, Y), lax.rem(c, Y)
    core = lax.rem(s, 2)
    mate = s + 1 - 2 * core
    ypeer = [z * Y + lax.rem(y + j, Y) for j in range(1, Y)]
    up, down = z < Z - 1, z > 0

    barrier = pltpu.get_barrier_semaphore()
    links = [(up, (s, c + Y)), (down, (s, c - Y))]
    links += [(None, (s, peer)) for peer in ypeer]
    links += [(None, (lax.rem(s + j, S), c)) for j in range(1, S)]
    targets = []
    pair = S // 2
    x = lax.div(s, 2)
    host = 2 * lax.rem(lax.div(c, 2), pair) + lax.rem(c, 2)
    for j in range(r):
        to = (host, s * r + j)
        targets.append((jnp.logical_or(to[0] != s, to[1] != c), to, j, j))
    sources = []
    for k in range(n // 2):
        frm = (lax.div(c, r), 2 * k + core)
        other = jnp.logical_or(frm[0] != s, frm[1] != c)
        sources.append((jnp.logical_and(other, x == k % pair), frm))
    links += [(t[0], t[1]) for t in targets] + sources
    for cond, peer in links:
        when(cond, functools.partial(pl.semaphore_signal, barrier, inc=1, device_id=peer,
                                     device_id_type=pl.DeviceIdType.MESH))
    peers = sum(1 if cond is None else cond.astype(jnp.int32) for cond, _ in links)
    pl.semaphore_wait(barrier, peers)

    sent = []

    def send(cond, src, dst, ssem, rsem, to):
        def make():
            return pltpu.make_async_remote_copy(src_ref=src, dst_ref=dst, send_sem=ssem, recv_sem=rsem,
                                                device_id=to, device_id_type=pl.DeviceIdType.MESH)
        when(cond, lambda: make().start())
        sent.append((cond, make))

    def arrive(cond, dst, sem):
        when(cond, lambda: pltpu.make_async_copy(dst, dst, sem).wait())

    def own(u):
        return x_ref.at[u // H, pl.ds(u % H * part, part)]

    def block(u, slot):
        return g_ref.at[u // H, pl.ds(1 + u % H * part, part), slot]

    def along(cond, u, slot, src, side):
        ok, to = (up, (s, c + Y)) if side == 0 else (down, (s, c - Y))
        send(both(cond, ok), src, block(u, slot), vsend.at[u, side, slot], vrecv.at[u, slot], to)

    def across(cond, u, slot, src):
        for j, peer in enumerate(ypeer):
            send(cond, src, block(u, slot), ysend.at[u, j, slot], vrecv.at[u, slot], (s, peer))

    def landed(cond, u, slot):
        arrive(cond, block(u, slot), vrecv.at[u, slot])

    def rim(cond, u, slot, first=None, last=None):
        v = u // H
        if u % H == H - 1:
            last = g_ref.at[v, planes, slot] if last is None else last
            send(both(cond, s < S - 1), last, g_ref.at[v, 0, slot], hsend.at[v, 0, slot], hrecv.at[v, 0, slot],
                 (s + 1, c))
        if u % H == 0:
            first = g_ref.at[v, 1, slot] if first is None else first
            send(both(cond, s > 0), first, g_ref.at[v, planes + 1, slot], hsend.at[v, 1, slot], hrecv.at[v, 1, slot],
                 (s - 1, c))

    for u in range(units):
        for side in range(2):
            along(None, u, c, own(u), side)
        across(None, u, c, own(u))
        if u == H - 1:
            for cond, to, j, k in targets:
                send(cond, p_ref.at[j], wg_ref.at[c], psend.at[k], precv.at[c], to)
    for j in range(1, S // 2):
        send(None, w_ref, wf_ref.at[s], wsend.at[j], wrecv.at[s], (lax.rem(s + 2 * j, S), c))
    send(None, w_ref, wf_ref.at[s], wsend.at[0], wrecv.at[s], (mate, c))
    for u in range(units):
        pltpu.make_async_copy(own(u), block(u, c), lsem.at[u]).start()
        rim(None, u, c, x_ref.at[u // H, 0], x_ref.at[u // H, planes - 1])
    pltpu.make_async_copy(w_ref, wf_ref.at[s], lsem.at[units]).start()
    home = jnp.logical_and(s == lax.div(c, r), s == host)
    when(home, lambda: pltpu.make_async_copy(p_ref.at[lax.rem(c, r)], wg_ref.at[c], precv.at[c]).start())

    for side in range(2):
        def clear(side=side):
            for v in range(2):
                row = 0 if side == 0 else planes + 1
                g_ref[v, row] = jnp.zeros(g_ref.shape[2:], g_ref.dtype)
        when(s == (0 if side == 0 else S - 1), clear)

    for k in range(1, Z):
        for u in range(units):
            for side in range(2):
                zz = z - k if side == 0 else z + k
                have = zz >= 0 if side == 0 else zz < Z
                slot = zz * Y + y
                landed(have, u, slot)
                if k < Z - 1:
                    along(have, u, slot, block(u, slot), side)
                across(have, u, slot, block(u, slot))
                rim(have, u, slot)
        if k == 1:
            for j in range(1, S // 2):
                slot = lax.rem(s + 2 * j, S)
                arrive(None, wf_ref.at[slot], wrecv.at[slot])
                send(None, wf_ref.at[slot], wf_ref.at[slot], wsend.at[S // 2 + j], wrecv.at[slot], (mate, c))
    for direct in range(2):
        for k in range(n // 2):
            slot = 2 * k + core
            have = x == k % pair if direct == 0 else x != k % pair
            piece = wg_ref.at[slot]
            arrive(have, piece, precv.at[slot])
            if direct == 0:
                for j in range(1, pair):
                    send(have, piece, piece, xsend.at[j, k], precv.at[slot], (lax.rem(s + 2 * j, S), c))
            send(have, piece, piece, fsend.at[k], precv.at[slot], (mate, c))
    for k in range(Z):
        for u in range(units):
            for peer in ypeer:
                for side in range(2 if k else 1):
                    zz = z - k if side == 0 else z + k
                    have = None if k == 0 else zz >= 0 if side == 0 else zz < Z
                    slot = zz * Y + peer - z * Y
                    landed(have, u, slot)
                    rim(have, u, slot)
    for u in range(units):
        pltpu.make_async_copy(own(u), block(u, c), lsem.at[u]).wait()
    pltpu.make_async_copy(w_ref, wf_ref.at[s], lsem.at[units]).wait()
    for j in range(S // 2):
        slot = lax.rem(mate + 2 * j, S)
        arrive(None, wf_ref.at[slot], wrecv.at[slot])
    for k in range(n // 2):
        slot = 2 * k + 1 - core
        arrive(None, wg_ref.at[slot], precv.at[slot])
    for v in range(2):
        for slot in range(n):
            arrive(s > 0, g_ref.at[v, 0, slot], hrecv.at[v, 0, slot])
            arrive(s < S - 1, g_ref.at[v, planes + 1, slot], hrecv.at[v, 1, slot])
    for cond, make in sent:
        when(cond, lambda make=make: make().wait_send())


def conv_kernel(g_ref, wf_ref, wg_ref, o_ref, k_ref):
    S, _, lc, width = wf_ref.shape
    n = wg_ref.shape[0]
    planes = o_ref.shape[1]
    cells = o_ref.shape[3]
    pack = LANES // lc
    for t in range(TAPS):
        rows = pl.ds(t * lc, lc)
        k_ref[0, rows, :] = jnp.concatenate([wf_ref[i, t] for i in range(S)], axis=-1)
        f = TAPS - 1 - t
        at = (f % pack) * lc
        k_ref[1, rows, :] = jnp.concatenate([wg_ref[i, f // pack][:, at:at + lc] for i in range(n)], axis=-1)
    lane = lax.broadcasted_iota(jnp.int32, (lc, cells), 1)
    row, col = lane // COLS, lane % COLS
    nine = 9 * lc

    def step(k, carry):
        v, d = k // planes, k % planes
        total = None
        for a in range(3):
            part = jnp.dot(k_ref[v, pl.ds(a * nine, nine), :], g_ref[v, d + a], preferred_element_type=jnp.float32)
            total = part if total is None else total + part
        result = None
        for b in range(3):
            lines = None
            for c in range(3):
                at = (3 * b + c) * lc
                piece = total[at:at + lc]
                if c != 1:
                    piece = pltpu.roll(piece, (1 - c) % cells, 1)
                    piece = jnp.where(col == (0 if c == 0 else COLS - 1), 0.0, piece)
                lines = piece if lines is None else lines + piece
            if b != 1:
                lines = pltpu.roll(lines, ((1 - b) * COLS) % cells, 1)
                lines = jnp.where(row == (0 if b == 0 else ROWS - 1), 0.0, lines)
            result = lines if result is None else result + lines
        o_ref[v, d] = result.astype(o_ref.dtype)
        return carry

    lax.fori_loop(0, 2 * planes, step, 0)


def body(S, n, inputs, weights, cotangent):
    lc, planes, cells = inputs.shape
    wide = weights.shape[2]
    r = wide // lc
    C = n * lc
    Y = max(d for d in range(1, n + 1) if n % d == 0 and 2 * d * d <= n)
    Z = n // Y
    volumes = jnp.stack((inputs, cotangent)).transpose(0, 2, 1, 3)
    pack = LANES // lc
    nt = -(-TAPS // pack)
    padded = jnp.pad(weights, ((0, nt * pack - TAPS), (0, 0), (0, 0)))
    pieces = padded.reshape(nt, pack, lc, r, lc).transpose(3, 0, 4, 1, 2).reshape(r, nt, lc, pack * lc)
    vmem = pl.BlockSpec(memory_space=pltpu.VMEM)
    anyspace = pl.BlockSpec(memory_space=pl.ANY)
    dma = pltpu.SemaphoreType.DMA
    bf16 = jnp.bfloat16
    gathered, wf, wg = pl.pallas_call(
        functools.partial(gather_kernel, S, Z, Y, r),
        out_shape=(jax.ShapeDtypeStruct((2, planes + 2, n, lc, cells), bf16),
                   jax.ShapeDtypeStruct((S,) + weights.shape, bf16),
                   jax.ShapeDtypeStruct((n,) + pieces.shape[1:], bf16)),
        in_specs=[anyspace] * 3,
        out_specs=(vmem,) * 3,
        scratch_shapes=[dma((2 * H + 1,)), dma((2 * H, 2, n)), dma((2 * H, Y - 1, n)), dma((2 * H, n)), dma((2, 2, n)), dma((2, 2, n)),
                        dma((S,)), dma((S,)), dma((r,)), dma((n // 2,)), dma((S // 2, n // 2)), dma((n,))],
        compiler_params=pltpu.CompilerParams(collective_id=0, has_side_effects=True, vmem_limit_bytes=40 << 20),
        name="gather",
    )(volumes, weights, pieces)
    out = pl.pallas_call(
        conv_kernel,
        out_shape=jax.ShapeDtypeStruct((2, planes, lc, cells), bf16),
        in_specs=[vmem] * 3,
        out_specs=vmem,
        scratch_shapes=[pltpu.VMEM((2, TAPS * lc, C), bf16)],
        compiler_params=pltpu.CompilerParams(vmem_limit_bytes=48 << 20),
        name="conv",
    )(gathered.reshape(2, planes + 2, C, cells), wf, wg)
    out = out.transpose(0, 2, 1, 3)
    return out[0], out[1]


def solution(mesh):
    S, n = mesh.shape["slab"], mesh.shape["chan"]
    return jax.shard_map(
        functools.partial(body, S, n),
        mesh=mesh,
        in_specs=(P("chan", "slab", None), P(None, "chan", "slab"), P("chan", "slab", None)),
        out_specs=(P("chan", "slab", None), P("chan", "slab", None)),
        check_vma=False,
    )
```
